32 devices in a mesh: gx: 16 (over z, y, core), gz: 2 (over x).
Axes of the slice: x: 2, y: 2, z: 4, core: 2. Of those that a mesh axis runs over, the one named last changes fastest.
Arguments:
- density: float32 [4096, 8, 1024], P('gx', None, 'gz'), may hold values from 0.5 to 2
- momentum: float32 [3, 4096, 8, 1024], P(None, 'gx', None, 'gz'), may hold values from -3 to 3
- energy: float32 [4096, 8, 1024], P('gx', None, 'gz'), may hold values from 2 to 4
- costate: float32 [5, 4096, 8, 1024], P(None, 'gx', None, 'gz'), may hold values from -6 to 6
Outputs:
- adjoint: float32 [5, 4096, 8, 1024], P(None, 'gx', None, 'gz')
The draws below stay inside these ranges and needn't reach their ends.
All inputs are finite; a program needn't handle non-finite values.
Results may differ from the reference program's by a relative error of at most 0.00005.
Values sent between devices are 32-bit elements; how exact they have to be, the bound alone decides.
A program may use at most 192 MiB of HBM per device.

```python
import math
import jax
import jax.numpy as jnp
from jax import lax

NX = 4096
NZ = 1024
NY = 8


def block_levels(rng, shape, pieces, low, top_value):
    def one(axis_at, blocks):
        heights = jax.random.uniform(jax.random.fold_in(jax.random.fold_in(rng, 6), axis_at), (blocks,), jnp.float32, low / len(pieces), top_value / len(pieces))
        return jnp.repeat(jnp.exp(heights), shape[axis_at] // blocks).reshape((-1,) + (1,) * (len(shape) - axis_at - 1))

    gain = one(*pieces[0])
    for cut in pieces[1:]:
        gain = gain * one(*cut)
    return gain


def normal_values(stream_key, dims, width, limit, pieces=(), kind=jnp.bfloat16):
    values = width * jax.random.normal(stream_key, dims, jnp.float32)
    if pieces:
        values = values * block_levels(stream_key, dims, pieces, -0.22, 0.18)
    return jnp.clip(values, -limit, limit).astype(kind)


def setup_inputs(seed: int = 0) -> dict:
    keys = jax.random.split(jax.random.key(seed), 5)
    density = jnp.clip(0.5 + 1.5 * jax.random.uniform(keys[0], (NX, NY, NZ), jnp.float32) ** block_levels(keys[0], (NX, NY, NZ), ((0, 16), (2, 2)), -0.2, 0.2), 0.5, 2.0)
    momentum = normal_values(keys[1], (3, NX, NY, NZ), 0.5, 3.0, ((1, 16), (3, 2)), jnp.float32)
    energy = jnp.clip(2.0 + 2.0 * jax.random.uniform(keys[2], (NX, NY, NZ), jnp.float32) ** block_levels(keys[2], (NX, NY, NZ), ((0, 16), (2, 2)), -0.2, 0.2), 2.0, 4.0)
    costate = normal_values(keys[3], (5, NX, NY, NZ), 1.0, 6.0, ((1, 16), (3, 2)), jnp.float32)
    return {"density": density, "momentum": momentum, "energy": energy, "costate": costate}


pade_alpha = 1.0 / 3.0
near_coef = 14.0 / 9.0
far_coef = 1.0 / 9.0
step_scale = 0.1
gas_gamma = 1.4

def fluxes(density, momentum, energy):
    inverse = 1.0 / density
    speed_stream = momentum[0] * inverse
    speed_span = momentum[2] * inverse
    kinetic = 0.5 * (momentum[0] * momentum[0] + momentum[1] * momentum[1] + momentum[2] * momentum[2]) * inverse
    pressure = (gas_gamma - 1.0) * (energy - kinetic)
    enthalpy = energy + pressure
    flux_stream = jnp.stack([momentum[0], momentum[0] * speed_stream + pressure, momentum[1] * speed_stream, momentum[2] * speed_stream, enthalpy * speed_stream])
    flux_span = jnp.stack([momentum[2], momentum[0] * speed_span, momentum[1] * speed_span, momentum[2] * speed_span + pressure, enthalpy * speed_span])
    return (flux_stream, flux_span)

def compact(values, line_axis):
    length = values.shape[line_axis]
    angles = 2.0 * math.pi * jnp.arange(length // 2 + 1) / length
    symbol = (near_coef * jnp.sin(angles) + 0.5 * far_coef * jnp.sin(2.0 * angles)) / (1.0 + 2.0 * pade_alpha * jnp.cos(angles))
    layout = [1, 1, 1]
    layout[line_axis] = length // 2 + 1
    spectrum = jnp.fft.rfft(values, axis=line_axis)
    return jnp.fft.irfft(spectrum * (1j * symbol).reshape(layout), n=length, axis=line_axis).astype(values.dtype)

def pullback(density, momentum, energy, slope_stream, slope_span):
    primal_out, pullback_fn = jax.vjp(fluxes, density, momentum, energy)
    gradients = pullback_fn((slope_stream, slope_span))
    return jnp.concatenate([gradients[0][None], gradients[1], gradients[2][None]], 0)

def reference(density, momentum, energy, costate):
    slope_stream = lax.map(lambda component: compact(component, 0), costate)
    slope_span = lax.map(lambda component: compact(component, 2), costate)

    def per_plane(plane_at):
        slab_of = lambda values: lax.dynamic_slice_in_dim(values, plane_at, 1, values.ndim - 2)
        result = pullback(slab_of(density), slab_of(momentum), slab_of(energy), slab_of(slope_stream), slab_of(slope_span))
        return result[:, :, 0, :]
    stacked = lax.map(per_plane, jnp.arange(NY, dtype=jnp.int32))
    pulled = jnp.transpose(stacked, (1, 2, 0, 3))
    return costate + step_scale * pulled
```

```python
import functools
import math

import jax
import jax.numpy as jnp
import numpy as np
from jax import lax
from jax.experimental import pallas as pl
from jax.experimental.pallas import tpu as pltpu
from jax.sharding import PartitionSpec as P

pade_alpha = 1.0 / 3.0
step_scale = 0.1
root = (-1.0 + math.sqrt(1.0 - 4.0 * pade_alpha * pade_alpha)) / (2.0 * pade_alpha)
near = step_scale / 12.0
tail = -step_scale * 25.0 / 12.0


def split(values):
    high = values.astype(jnp.bfloat16)
    low = (values - high.astype(jnp.float32)).astype(jnp.bfloat16)
    return high, low


def toeplitz(size):
    gap = np.arange(size)[:, None] - np.arange(size)[None, :]
    weight = tail * np.power(-root, np.abs(gap)) * np.where(gap % 2 == 0, 1.0, -1.0)
    weight = weight + near * (np.abs(gap) == 1)
    return np.sign(gap) * weight


def span_weights(length):
    block = min(256, length)
    inside = toeplitz(block)
    half = np.arange(block) < block // 2
    corner = inside * (half[:, None] != half[None, :])
    both = jnp.asarray(np.stack([inside, corner]).astype(np.float32))
    return jnp.stack(split(both))


def summary_weights():
    lane = np.arange(128)
    signed = lambda power: np.power(-root, power) * np.where(power % 2 == 0, 1.0, -1.0)
    rows = np.zeros((2, 8, 128), np.float32)
    rows[0, 0] = signed(lane + 1)
    rows[0, 1, 0] = 1.0
    rows[1, 0] = signed(128 - lane)
    rows[1, 1, 127] = 1.0
    return jnp.concatenate(split(jnp.asarray(rows)), 1)


def rim_weights():
    lane = np.arange(128)
    signed = lambda power: np.power(-root, power) * np.where(power % 2 == 0, 1.0, -1.0)
    rows = np.zeros((4, 256), np.float32)
    rows[0, :128] = -tail * signed(lane)
    rows[1, 0] = -near
    rows[2, 128:] = tail * signed(127 - lane)
    rows[3, 255] = near
    high, low = split(jnp.asarray(rows))
    return jnp.concatenate([high, high, low, jnp.zeros_like(high)])


def heard(chunks, rows):
    return [k for k in range(chunks) if abs(root ** (rows * k)) > 1e-38]


def decay(rows, k, at):
    scale = jnp.float32(0.0)
    for n in k:
        scale = jnp.where(at == n, jnp.float32(root ** (rows * n)), scale)
    return scale


def visit(step, chunks):
    return jnp.where(step % 2 == 0, chunks - 1 - step // 2, step // 2)


def edges_kernel(
    chunks, rows, cost_ref, weight_ref, raw_ref,
    ahead_ref, left_ref, right_ref, zleft_ref, zright_ref,
    up_ref, down_ref, local_ref, far_ref, zup_ref, zdown_ref, send, recv,
):
    step = pl.program_id(0)
    fields = cost_ref.shape[0]
    lanes = cost_ref.shape[3]
    length = raw_ref.shape[1]
    near_rows = heard(chunks, rows)
    ready = min(2 * len(near_rows), chunks)

    def shifted(axis, by):
        peers = lax.axis_size(axis)
        return {axis: lax.rem(lax.axis_index(axis) + (by + peers), peers)}

    after, before = shifted("gx", 1), shifted("gx", -1)
    zafter, zbefore = shifted("gz", 1), shifted("gz", -1)

    def remote(source, target, k, device):
        return pltpu.make_async_remote_copy(
            src_ref=source, dst_ref=target, send_sem=send.at[k], recv_sem=recv.at[k],
            device_id=device, device_id_type=pl.DeviceIdType.MESH,
        )

    rim_copies = [
        remote(raw_ref.at[:, length - 1], left_ref.at[1], 0, after),
        remote(raw_ref.at[:, 0], right_ref, 1, before),
    ]
    state_copies = [
        remote(up_ref, left_ref.at[0], 2, after),
        remote(down_ref, far_ref, 3, before),
    ]

    def span_copies(at):
        chunk = visit(at, chunks)
        return [
            remote(zup_ref.at[chunk], zleft_ref.at[chunk], 4 + at, zafter),
            remote(zdown_ref.at[chunk], zright_ref.at[chunk], 4 + chunks + at, zbefore),
        ]

    @pl.when(step == 0)
    def _():
        barrier = pltpu.get_barrier_semaphore()
        for device in (after, before, zafter, zbefore):
            pl.semaphore_signal(
                barrier, inc=1, device_id=device, device_id_type=pl.DeviceIdType.MESH
            )
        up_ref[...] = jnp.zeros_like(up_ref)
        down_ref[...] = jnp.zeros_like(down_ref)

    @pl.when(step == 1)
    def _():
        pl.semaphore_wait(pltpu.get_barrier_semaphore(), 4)
        for copy in rim_copies:
            copy.start()

    @pl.when(step >= 1)
    def _():
        for copy in span_copies(step - 1):
            copy.start()

    @pl.when(step == ready)
    def _():
        for copy in state_copies:
            copy.start()

    @pl.when(step < chunks)
    def _():
        chunk = visit(step, chunks)
        from_end = chunks - 1 - chunk

        @pl.when(from_end < len(near_rows))
        def _():
            scale = decay(rows, near_rows, from_end)
            fronts = [jnp.zeros_like(up_ref[f]) for f in range(fields)]
            for i in range(rows):
                fronts = [root * (cost_ref[f, i] + fronts[f]) for f in range(fields)]
            for f in range(fields):
                up_ref[f] = up_ref[f] + scale * fronts[f]

        contract = functools.partial(
            lax.dot_general, dimension_numbers=(((1,), (1,)), ((), ())),
            preferred_element_type=jnp.float32,
        )
        backs = [jnp.zeros_like(down_ref[f]) for f in range(fields)]
        for i in reversed(range(rows)):
            backs = [root * (cost_ref[f, i] + backs[f]) for f in range(fields)]
        scale = decay(rows, near_rows, chunk)
        for field in range(fields):
            local_ref[chunk, field] = backs[field]

            @pl.when(chunk < len(near_rows))
            def _():
                down_ref[field] = down_ref[field] + scale * backs[field]

            at = pl.ds(field * rows * 8, rows * 8)
            for side, from_lane, ref in ((0, 0, zdown_ref), (1, lanes - 128, zup_ref)):
                part = cost_ref[field, :, :, from_lane : from_lane + 128]
                high, low = split(part.reshape(rows * 8, 128))
                both = contract(weight_ref[side], high)
                ref[chunk, :, at] = (
                    both[0:2] + both[8:10] + contract(weight_ref[side], low)[0:2]
                )

    @pl.when(step == chunks)
    def _():
        for copy in rim_copies + state_copies:
            copy.wait()
        for f in range(fields):
            state = far_ref[f]
            ahead_ref[chunks - 1, f] = state
            for k in reversed(range(chunks - 1)):
                state = local_ref[k + 1, f] + (root**rows) * state
                ahead_ref[k, f] = state
        for at in range(chunks):
            for copy in span_copies(at):
                copy.wait()


def edges(costate, rows):
    fields, length, planes, lanes = costate.shape
    chunks = length // rows
    flat = fields * rows * planes
    layer = (fields, planes, lanes)
    f32 = jnp.float32
    anywhere = pl.BlockSpec(memory_space=pl.ANY)
    return pl.pallas_call(
        functools.partial(edges_kernel, chunks, rows),
        grid=(chunks + 1,),
        in_specs=[
            pl.BlockSpec(
                (fields, rows, planes, lanes),
                lambda s: (0, visit(jnp.minimum(s, chunks - 1), chunks), 0, 0),
            ),
            pl.BlockSpec((2, 16, 128), lambda s: (0, 0, 0)),
            anywhere,
        ],
        out_specs=[
            pl.BlockSpec((chunks,) + layer, lambda s: (0, 0, 0, 0)),
            anywhere, anywhere, anywhere, anywhere,
        ],
        out_shape=[
            jax.ShapeDtypeStruct((chunks,) + layer, f32),
            jax.ShapeDtypeStruct((2,) + layer, f32),
            jax.ShapeDtypeStruct(layer, f32),
            jax.ShapeDtypeStruct((chunks, 2, flat), f32),
            jax.ShapeDtypeStruct((chunks, 2, flat), f32),
        ],
        scratch_shapes=[
            pltpu.VMEM(layer, f32),
            pltpu.VMEM(layer, f32),
            pltpu.VMEM((chunks,) + layer, f32),
            pltpu.VMEM(layer, f32),
            pltpu.VMEM((chunks, 2, flat), f32),
            pltpu.VMEM((chunks, 2, flat), f32),
            pltpu.SemaphoreType.DMA((4 + 2 * chunks,)),
            pltpu.SemaphoreType.DMA((4 + 2 * chunks,)),
        ],
        compiler_params=pltpu.CompilerParams(collective_id=0, has_side_effects=True),
        name="edges",
    )(costate, summary_weights(), costate)


def pulled_back(density, momentum, energy, a, b):
    inverse = 1.0 / density
    u, v, w = (m * inverse for m in momentum)
    square = u * u + v * v + w * w
    fifth = 0.2 * square
    h = 1.4 * (energy * inverse) - fifth
    along = a[1] * u + a[2] * v + a[3] * w + a[4] * h
    across = b[1] * u + b[2] * v + b[3] * w + b[4] * h
    work = a[4] * u + b[4] * w
    push = work + a[1] + b[3]
    q = 0.4 * push
    return (
        fifth * push - (u * along + w * across),
        a[0] + along + (a[1] - q) * u + b[1] * w,
        a[2] * u + b[2] * w - q * v,
        b[0] + across + a[3] * u + (b[3] - q) * w,
        work + q,
    )


def main_kernel(
    chunks, rows, density_ref, momentum_ref, energy_ref, cost_ref, next_ref, ahead_ref,
    left_ref, right_ref, zleft_ref, zright_ref, weight_ref, rim_ref,
    out_ref, back_ref, span_ref, carry_ref,
):
    step = pl.program_id(0)
    fields, _, planes, lanes = cost_ref.shape
    block = weight_ref.shape[2]
    f32 = jnp.float32

    @pl.when(step == 0)
    def _():
        carry_ref[...] = left_ref[...]

    last = step == chunks - 1

    def times(high, low, kind):
        dot = functools.partial(jnp.dot, preferred_element_type=f32)
        heavy, light = weight_ref[0, kind], weight_ref[1, kind]
        return dot(high, heavy) + dot(low, heavy) + dot(high, light)

    flat = rows * planes
    turned = (((0,), (0,)), ((), ()))
    rim = jnp.concatenate([zleft_ref[0], zright_ref[0]], 0)
    rim_high = rim.astype(jnp.bfloat16).astype(f32)
    rim = jnp.concatenate([rim_high, rim - rim_high, rim_high, jnp.zeros_like(rim)], 0)
    rim = rim.astype(jnp.bfloat16)
    for field in range(fields):
        high, low = split(cost_ref[field].reshape(flat, lanes))
        tiles = []
        for at in range(0, lanes, block):
            part = times(high[:, at : at + block], low[:, at : at + block], 0)
            tiles += [part[:, t : t + 128] for t in range(0, block, 128)]
        for at in range(block // 2, lanes - block // 2, block):
            if at + block > lanes:
                break
            part = times(high[:, at : at + block], low[:, at : at + block], 1)
            for t in range(0, block, 128):
                tiles[(at + t) // 128] += part[:, t : t + 128]
        at = field * flat
        part = lax.dot_general(
            rim[:, at : at + flat], rim_ref[...], turned, preferred_element_type=f32
        )
        tiles[0] += part[:, :128]
        tiles[-1] += part[:, 128:]
        for t, tile in enumerate(tiles):
            span_ref[field, :, :, t * 128 : (t + 1) * 128] = tile.reshape(rows, planes, 128)
        back = ahead_ref[0, field]
        ahead = jnp.where(last, right_ref[field], next_ref[field, 0])
        for i in reversed(range(rows)):
            back_ref[field, i] = tail * back + near * ahead
            ahead = cost_ref[field, i]
            back = root * (ahead + back)

    for t in range(lanes // 128):
        at = slice(t * 128, (t + 1) * 128)

        def body(i, carried):
            fronts, befores = carried
            here = [cost_ref[f, i, :, at] for f in range(fields)]
            a = [
                back_ref[f, i, :, at] - (tail * fronts[f] + near * befores[f])
                for f in range(fields)
            ]
            b = [span_ref[f, i, :, at] for f in range(fields)]
            pulled = pulled_back(
                density_ref[i, :, at],
                [momentum_ref[k, i, :, at] for k in range(3)],
                energy_ref[i, :, at],
                a, b,
            )
            for f in range(fields):
                out_ref[f, i, :, at] = here[f] + pulled[f]
            return ([root * (p + q) for p, q in zip(here, fronts)], here)

        start = (
            [carry_ref[0, f, :, at] for f in range(fields)],
            [carry_ref[1, f, :, at] for f in range(fields)],
        )
        fronts, befores = lax.fori_loop(0, rows, body, start, unroll=8)
        for f in range(fields):
            carry_ref[0, f, :, at] = fronts[f]
            carry_ref[1, f, :, at] = befores[f]


def main(density, momentum, energy, costate, ahead, left, right, zleft, zright, rows):
    fields, length, planes, lanes = costate.shape
    chunks = length // rows
    flat = fields * rows * planes
    layer = (2, fields, planes, lanes)
    weights, rim = span_weights(lanes), rim_weights()
    whole = lambda array: pl.BlockSpec(array.shape, lambda s: (0,) * array.ndim)
    state = pl.BlockSpec((rows, planes, lanes), lambda s: (s, 0, 0))
    stacked = lambda k: pl.BlockSpec((k, rows, planes, lanes), lambda s: (0, s, 0, 0))
    strip = pl.BlockSpec((1, 2, flat), lambda s: (s, 0, 0))
    f32 = jnp.float32
    return pl.pallas_call(
        functools.partial(main_kernel, chunks, rows),
        grid=(chunks,),
        in_specs=[
            state, stacked(3), state, stacked(fields),
            pl.BlockSpec(
                (fields, 1, planes, lanes),
                lambda s: (0, jnp.minimum(rows * (s + 1), length - 1), 0, 0),
            ),
            pl.BlockSpec((1,) + layer[1:], lambda s: (s, 0, 0, 0)),
            whole(left), whole(right), strip, strip, whole(weights), whole(rim),
        ],
        out_specs=stacked(fields),
        out_shape=jax.ShapeDtypeStruct(costate.shape, f32),
        scratch_shapes=[
            pltpu.VMEM((fields, rows, planes, lanes), f32),
            pltpu.VMEM((fields, rows, planes, lanes), f32),
            pltpu.VMEM(layer, f32),
        ],
        name="pull",
    )(density, momentum, energy, costate, costate, ahead, left, right, zleft, zright, weights, rim)


def per_device(density, momentum, energy, costate):
    rows = 32
    ahead, left, right, zleft, zright = edges(costate, rows)
    return main(density, momentum, energy, costate, ahead, left, right, zleft, zright, rows)


def solution(mesh):
    return jax.shard_map(
        per_device,
        mesh=mesh,
        in_specs=(
            P("gx", None, "gz"),
            P(None, "gx", None, "gz"),
            P("gx", None, "gz"),
            P(None, "gx", None, "gz"),
        ),
        out_specs=P(None, "gx", None, "gz"),
        check_vma=False,
    )
```

```python
import functools
import math

import jax
import jax.numpy as jnp
import numpy as np
from jax import lax
from jax.experimental import pallas as pl
from jax.experimental.pallas import tpu as pltpu
from jax.sharding import PartitionSpec as P

pade_alpha = 1.0 / 3.0
step_scale = 0.1
root = (-1.0 + math.sqrt(1.0 - 4.0 * pade_alpha * pade_alpha)) / (2.0 * pade_alpha)
near = step_scale / 12.0
tail = -step_scale * 25.0 / 12.0


def split(values):
    high = values.astype(jnp.bfloat16)
    low = (values - high.astype(jnp.float32)).astype(jnp.bfloat16)
    return high, low


def toeplitz(size):
    gap = np.arange(size)[:, None] - np.arange(size)[None, :]
    weight = tail * np.power(-root, np.abs(gap)) * np.where(gap % 2 == 0, 1.0, -1.0)
    weight = weight + near * (np.abs(gap) == 1)
    return np.sign(gap) * weight


def span_weights(length):
    block = min(256, length)
    inside = toeplitz(block)
    half = np.arange(block) < block // 2
    corner = inside * (half[:, None] != half[None, :])
    both = jnp.asarray(np.stack([inside, corner]).astype(np.float32))
    return jnp.stack(split(both))


def summary_weights():
    lane = np.arange(128)
    signed = lambda power: np.power(-root, power) * np.where(power % 2 == 0, 1.0, -1.0)
    rows = np.zeros((2, 8, 128), np.float32)
    rows[0, 0] = signed(lane + 1)
    rows[0, 1, 0] = 1.0
    rows[1, 0] = signed(128 - lane)
    rows[1, 1, 127] = 1.0
    return jnp.concatenate(split(jnp.asarray(rows)), 1)


def rim_weights():
    lane = np.arange(128)
    signed = lambda power: np.power(-root, power) * np.where(power % 2 == 0, 1.0, -1.0)
    rows = np.zeros((4, 256), np.float32)
    rows[0, :128] = -tail * signed(lane)
    rows[1, 0] = -near
    rows[2, 128:] = tail * signed(127 - lane)
    rows[3, 255] = near
    high, low = split(jnp.asarray(rows))
    return jnp.concatenate([high, high, low, jnp.zeros_like(high)])


def heard(chunks, rows):
    return [k for k in range(chunks) if abs(root ** (rows * k)) > 1e-38]


def decay(rows, k, at):
    scale = jnp.float32(0.0)
    for n in k:
        scale = jnp.where(at == n, jnp.float32(root ** (rows * n)), scale)
    return scale


def visit(step, chunks):
    return jnp.where(step % 2 == 0, chunks - 1 - step // 2, step // 2)


def edges_kernel(
    chunks, rows, cost_ref, first_ref, final_ref, weight_ref, raw_ref,
    ahead_ref, left_ref, right_ref, zleft_ref, zright_ref,
    up_ref, down_ref, local_ref, far_ref, zup_ref, zdown_ref, send, recv,
):
    step = pl.program_id(0)
    fields = cost_ref.shape[0]
    length = raw_ref.shape[1]
    near_rows = heard(chunks, rows)
    ready = min(2 * len(near_rows), chunks)

    def shifted(axis, by):
        peers = lax.axis_size(axis)
        return {axis: lax.rem(lax.axis_index(axis) + (by + peers), peers)}

    after, before = shifted("gx", 1), shifted("gx", -1)
    zafter, zbefore = shifted("gz", 1), shifted("gz", -1)

    def remote(source, target, k, device):
        return pltpu.make_async_remote_copy(
            src_ref=source, dst_ref=target, send_sem=send.at[k], recv_sem=recv.at[k],
            device_id=device, device_id_type=pl.DeviceIdType.MESH,
        )

    rim_copies = [
        remote(raw_ref.at[:, length - 1], left_ref.at[1], 0, after),
        remote(raw_ref.at[:, 0], right_ref, 1, before),
    ]
    state_copies = [
        remote(up_ref, left_ref.at[0], 2, after),
        remote(down_ref, far_ref, 3, before),
    ]

    def span_copies(at):
        return [
            remote(zup_ref.at[at], zleft_ref.at[at], 4 + at, zafter),
            remote(zdown_ref.at[at], zright_ref.at[at], 4 + chunks + at, zbefore),
        ]

    @pl.when(step == 0)
    def _():
        barrier = pltpu.get_barrier_semaphore()
        for device in (after, before, zafter, zbefore):
            pl.semaphore_signal(
                barrier, inc=1, device_id=device, device_id_type=pl.DeviceIdType.MESH
            )
        up_ref[...] = jnp.zeros_like(up_ref)
        down_ref[...] = jnp.zeros_like(down_ref)

    @pl.when(step == 1)
    def _():
        pl.semaphore_wait(pltpu.get_barrier_semaphore(), 4)
        for copy in rim_copies:
            copy.start()

    @pl.when(step > chunks)
    def _():
        for copy in span_copies(step - 1 - chunks):
            copy.start()

    @pl.when(step == ready)
    def _():
        for copy in state_copies:
            copy.start()

    @pl.when(step < chunks)
    def _():
        chunk = visit(step, chunks)
        from_end = chunks - 1 - chunk

        @pl.when(from_end < len(near_rows))
        def _():
            scale = decay(rows, near_rows, from_end)
            fronts = [jnp.zeros_like(up_ref[f]) for f in range(fields)]
            for i in range(rows):
                fronts = [root * (cost_ref[f, i] + fronts[f]) for f in range(fields)]
            for f in range(fields):
                up_ref[f] = up_ref[f] + scale * fronts[f]

        backs = [jnp.zeros_like(down_ref[f]) for f in range(fields)]
        for i in reversed(range(rows)):
            backs = [root * (cost_ref[f, i] + backs[f]) for f in range(fields)]
        scale = decay(rows, near_rows, chunk)
        for field in range(fields):
            local_ref[chunk, field] = backs[field]

            @pl.when(chunk < len(near_rows))
            def _():
                down_ref[field] = down_ref[field] + scale * backs[field]

    @pl.when((step >= chunks) & (step < 2 * chunks))
    def _():
        chunk = step - chunks
        contract = functools.partial(
            lax.dot_general, dimension_numbers=(((1,), (1,)), ((), ())),
            preferred_element_type=jnp.float32,
        )
        for field in range(fields):
            at = slice(field * rows * 8, (field + 1) * rows * 8)
            for side, edge, ref in ((0, first_ref, zdown_ref), (1, final_ref, zup_ref)):
                high, low = split(edge[field].reshape(rows * 8, 128))
                both = contract(weight_ref[side], high)
                ref[chunk, :, at] = (
                    both[0:2] + both[8:10] + contract(weight_ref[side], low)[0:2]
                )

    @pl.when(step == 2 * chunks)
    def _():
        for copy in rim_copies + state_copies:
            copy.wait()
        for f in range(fields):
            state = far_ref[f]
            ahead_ref[chunks - 1, f] = state
            for k in reversed(range(chunks - 1)):
                state = local_ref[k + 1, f] + (root**rows) * state
                ahead_ref[k, f] = state
        for at in range(chunks):
            for copy in span_copies(at):
                copy.wait()


def edges(costate, rows):
    fields, length, planes, lanes = costate.shape
    chunks = length // rows
    flat = fields * rows * planes
    layer = (fields, planes, lanes)
    f32 = jnp.float32
    anywhere = pl.BlockSpec(memory_space=pl.ANY)
    later = lambda s: jnp.clip(s - chunks, 0, chunks - 1)
    edge = lambda tile: pl.BlockSpec(
        (fields, rows, planes, 128), lambda s: (0, later(s), 0, tile)
    )
    return pl.pallas_call(
        functools.partial(edges_kernel, chunks, rows),
        grid=(2 * chunks + 1,),
        in_specs=[
            pl.BlockSpec(
                (fields, rows, planes, lanes),
                lambda s: (0, visit(jnp.minimum(s, chunks - 1), chunks), 0, 0),
            ),
            edge(0), edge(lanes // 128 - 1),
            pl.BlockSpec((2, 16, 128), lambda s: (0, 0, 0)),
            anywhere,
        ],
        out_specs=[
            pl.BlockSpec((chunks,) + layer, lambda s: (0, 0, 0, 0)),
            anywhere, anywhere, anywhere, anywhere,
        ],
        out_shape=[
            jax.ShapeDtypeStruct((chunks,) + layer, f32),
            jax.ShapeDtypeStruct((2,) + layer, f32),
            jax.ShapeDtypeStruct(layer, f32),
            jax.ShapeDtypeStruct((chunks, 2, flat), f32),
            jax.ShapeDtypeStruct((chunks, 2, flat), f32),
        ],
        scratch_shapes=[
            pltpu.VMEM(layer, f32),
            pltpu.VMEM(layer, f32),
            pltpu.VMEM((chunks,) + layer, f32),
            pltpu.VMEM(layer, f32),
            pltpu.VMEM((chunks, 2, flat), f32),
            pltpu.VMEM((chunks, 2, flat), f32),
            pltpu.SemaphoreType.DMA((4 + 2 * chunks,)),
            pltpu.SemaphoreType.DMA((4 + 2 * chunks,)),
        ],
        compiler_params=pltpu.CompilerParams(collective_id=0, has_side_effects=True),
        name="edges",
    )(costate, costate, costate, summary_weights(), costate)


def pulled_back(density, momentum, energy, a, b):
    inverse = 1.0 / density
    u, v, w = (m * inverse for m in momentum)
    square = u * u + v * v + w * w
    fifth = 0.2 * square
    h = 1.4 * (energy * inverse) - fifth
    along = a[1] * u + a[2] * v + a[3] * w + a[4] * h
    across = b[1] * u + b[2] * v + b[3] * w + b[4] * h
    work = a[4] * u + b[4] * w
    push = work + a[1] + b[3]
    q = 0.4 * push
    return (
        fifth * push - (u * along + w * across),
        a[0] + along + (a[1] - q) * u + b[1] * w,
        a[2] * u + b[2] * w - q * v,
        b[0] + across + a[3] * u + (b[3] - q) * w,
        work + q,
    )


def main_kernel(
    chunks, rows, density_ref, momentum_ref, energy_ref, cost_ref, next_ref, ahead_ref,
    left_ref, right_ref, zleft_ref, zright_ref, weight_ref, rim_ref,
    out_ref, back_ref, span_ref, carry_ref,
):
    step = pl.program_id(0)
    fields, _, planes, lanes = cost_ref.shape
    block = weight_ref.shape[2]
    f32 = jnp.float32

    @pl.when(step == 0)
    def _():
        carry_ref[...] = left_ref[...]

    last = step == chunks - 1

    def times(high, low, kind):
        dot = functools.partial(jnp.dot, preferred_element_type=f32)
        heavy, light = weight_ref[0, kind], weight_ref[1, kind]
        return dot(high, heavy) + dot(low, heavy) + dot(high, light)

    flat = rows * planes
    turned = (((0,), (0,)), ((), ()))
    rim = jnp.concatenate([zleft_ref[0], zright_ref[0]], 0)
    rim_high = rim.astype(jnp.bfloat16).astype(f32)
    rim = jnp.concatenate([rim_high, rim - rim_high, rim_high, jnp.zeros_like(rim)], 0)
    rim = rim.astype(jnp.bfloat16)
    for field in range(fields):
        high, low = split(cost_ref[field].reshape(flat, lanes))
        tiles = []
        for at in range(0, lanes, block):
            part = times(high[:, at : at + block], low[:, at : at + block], 0)
            tiles += [part[:, t : t + 128] for t in range(0, block, 128)]
        for at in range(block // 2, lanes - block // 2, block):
            if at + block > lanes:
                break
            part = times(high[:, at : at + block], low[:, at : at + block], 1)
            for t in range(0, block, 128):
                tiles[(at + t) // 128] += part[:, t : t + 128]
        at = field * flat
        part = lax.dot_general(
            rim[:, at : at + flat], rim_ref[...], turned, preferred_element_type=f32
        )
        tiles[0] += part[:, :128]
        tiles[-1] += part[:, 128:]
        for t, tile in enumerate(tiles):
            span_ref[field, :, :, t * 128 : (t + 1) * 128] = tile.reshape(rows, planes, 128)
        back = ahead_ref[0, field]
        ahead = jnp.where(last, right_ref[field], next_ref[field, 0])
        for i in reversed(range(rows)):
            back_ref[field, i] = tail * back + near * ahead
            ahead = cost_ref[field, i]
            back = root * (ahead + back)

    for t in range(lanes // 128):
        at = slice(t * 128, (t + 1) * 128)

        def body(i, carried):
            fronts, befores = carried
            here = [cost_ref[f, i, :, at] for f in range(fields)]
            a = [
                back_ref[f, i, :, at] - (tail * fronts[f] + near * befores[f])
                for f in range(fields)
            ]
            b = [span_ref[f, i, :, at] for f in range(fields)]
            pulled = pulled_back(
                density_ref[i, :, at],
                [momentum_ref[k, i, :, at] for k in range(3)],
                energy_ref[i, :, at],
                a, b,
            )
            for f in range(fields):
                out_ref[f, i, :, at] = here[f] + pulled[f]
            return ([root * (p + q) for p, q in zip(here, fronts)], here)

        start = (
            [carry_ref[0, f, :, at] for f in range(fields)],
            [carry_ref[1, f, :, at] for f in range(fields)],
        )
        fronts, befores = lax.fori_loop(0, rows, body, start, unroll=8)
        for f in range(fields):
            carry_ref[0, f, :, at] = fronts[f]
            carry_ref[1, f, :, at] = befores[f]


def main(density, momentum, energy, costate, ahead, left, right, zleft, zright, rows):
    fields, length, planes, lanes = costate.shape
    chunks = length // rows
    flat = fields * rows * planes
    layer = (2, fields, planes, lanes)
    weights, rim = span_weights(lanes), rim_weights()
    whole = lambda array: pl.BlockSpec(array.shape, lambda s: (0,) * array.ndim)
    state = pl.BlockSpec((rows, planes, lanes), lambda s: (s, 0, 0))
    stacked = lambda k: pl.BlockSpec((k, rows, planes, lanes), lambda s: (0, s, 0, 0))
    strip = pl.BlockSpec((1, 2, flat), lambda s: (s, 0, 0))
    f32 = jnp.float32
    return pl.pallas_call(
        functools.partial(main_kernel, chunks, rows),
        grid=(chunks,),
        in_specs=[
            state, stacked(3), state, stacked(fields),
            pl.BlockSpec(
                (fields, 1, planes, lanes),
                lambda s: (0, jnp.minimum(rows * (s + 1), length - 1), 0, 0),
            ),
            pl.BlockSpec((1,) + layer[1:], lambda s: (s, 0, 0, 0)),
            whole(left), whole(right), strip, strip, whole(weights), whole(rim),
        ],
        out_specs=stacked(fields),
        out_shape=jax.ShapeDtypeStruct(costate.shape, f32),
        scratch_shapes=[
            pltpu.VMEM((fields, rows, planes, lanes), f32),
            pltpu.VMEM((fields, rows, planes, lanes), f32),
            pltpu.VMEM(layer, f32),
        ],
        name="pull",
    )(density, momentum, energy, costate, costate, ahead, left, right, zleft, zright, weights, rim)


def per_device(density, momentum, energy, costate):
    rows = 32
    ahead, left, right, zleft, zright = edges(costate, rows)
    return main(density, momentum, energy, costate, ahead, left, right, zleft, zright, rows)


def solution(mesh):
    return jax.shard_map(
        per_device,
        mesh=mesh,
        in_specs=(
            P("gx", None, "gz"),
            P(None, "gx", None, "gz"),
            P("gx", None, "gz"),
            P(None, "gx", None, "gz"),
        ),
        out_specs=P(None, "gx", None, "gz"),
        check_vma=False,
    )
```
